128 devices in a mesh: row: 8 (over x, core), col: 16 (over z, y).
Axes of the slice: x: 4, y: 4, z: 4, core: 2. Of those that a mesh axis runs over, the one named last changes fastest.
Arguments:
- tokens: bfloat16 [7168, 4096], P('col', 'row'), may hold values from -50 to 50
- ln_gain: float32 [4096], P('row'), may hold values from 0.1 to 1.9
- ln_shift: float32 [4096], P('row'), may hold values from -4 to 4
- w_qkv: bfloat16 [4096, 12288], P('row', 'col'), may hold values from -2 to 2
- w_out: bfloat16 [4096, 4096], P('col', 'row'), may hold values from -0.09375 to 0.09375
- layer_scale: float32 [4096], P('row'), may hold values from 0.5 to 2
- segments: int32 [7168], replicated, may hold values from 0 to 16, as said below
- present: int32 [7168], replicated, may hold values from 0 to 1, as said below
- coords: int32 [2, 7168], replicated, may hold values from 0 to 22, as said below
- owner_slot: int32 [7168], replicated, may hold values from 0 to 7167, as said below
Outputs:
- layer_out: bfloat16 [7168, 4096], P('col', 'row')
The draws below stay inside these ranges and needn't reach their ends.
Inputs may be any that keep to these rules, and one draw needn't show every extreme that they name: `segments`: the picture of each token, pictures numbered in stream order; each picture's tokens form one run, pictures follow each other from position 0, and the padding tokens after them carry 16. `present`: 1 exactly where segments is below 16. A picture has h rows of w patches, 8 <= h <= 18 and 12 <= w <= 22, and some picture has 18 rows of 22; its first 5 tokens (class and registers) have 0 in both rows of coords, then its patches follow in row-major order with patch row and column counted from 1; padding tokens have 0 in both. `owner_slot`: A permutation of the 7168 tokens onto slots. Each block of 896 slots (slot // 896) holds 2 whole pictures, each on consecutive slots in stream order, followed by padding tokens.
All inputs are finite; a program needn't handle non-finite values.
Results may differ from the reference program's by a relative error of at most 0.017.
Values may be sent and summed in bfloat16 or wider, within the bound.
A program may use at most 64 MiB of HBM per device.

```python
import math
import jax
import jax.numpy as jnp
from jax import lax

D = 4096
HEADS = 32
HD = 128
IMG_ROW = 2
PREFIX = 5
HMIN = 8
HMAX = 18
WMIN = 12
WMAX = 22
TOK_ROW = 896
IMAGES = 16
TOKENS = 7168
N_ROW = 8


def layout(key):
    base_key = jax.random.fold_in(key, 7)
    height_key, width_key, order_key = jax.random.split(base_key, 3)
    heights = jax.random.randint(height_key, (IMAGES,), HMIN, HMAX + 1).astype(jnp.int32).at[0].set(HMAX)
    widths = jax.random.randint(width_key, (IMAGES,), WMIN, WMAX + 1).astype(jnp.int32).at[0].set(WMAX)
    lengths = PREFIX + heights * widths
    placing = jax.random.permutation(order_key, IMAGES).astype(jnp.int32)
    holder = placing // IMG_ROW
    earlier = (holder[None, :] == holder[:, None]) & (placing[None, :] < placing[:, None])
    offset = jnp.sum(jnp.where(earlier, lengths[None, :], 0), axis=1)
    group_ids = jnp.arange(N_ROW, dtype=jnp.int32)
    filled = jnp.sum(jnp.where(holder[None, :] == group_ids[:, None], lengths[None, :], 0), axis=1)
    stream_start = jnp.cumsum(lengths) - lengths
    real_total = jnp.sum(lengths)
    position = jnp.arange(TOKENS, dtype=jnp.int32)
    picture = jnp.sum((position[:, None] >= stream_start[None, :]).astype(jnp.int32), axis=1) - 1
    is_real = position < real_total
    within = position - stream_start[picture]
    real_slot = holder[picture] * TOK_ROW + offset[picture] + within
    leftover = TOK_ROW - filled
    leftover_start = jnp.cumsum(leftover) - leftover
    pad_index = position - real_total
    pad_group = jnp.sum((pad_index[:, None] >= leftover_start[None, :]).astype(jnp.int32), axis=1) - 1
    pad_group = jnp.clip(pad_group, 0, N_ROW - 1)
    pad_slot = pad_group * TOK_ROW + filled[pad_group] + pad_index - leftover_start[pad_group]
    target = jnp.where(is_real, real_slot, pad_slot).astype(jnp.int32)
    patch_index = within - PREFIX
    on_grid = is_real & (patch_index >= 0)
    safe_patch = jnp.maximum(patch_index, 0)
    row_pos = jnp.where(on_grid, safe_patch // widths[picture] + 1, 0).astype(jnp.int32)
    col_pos = jnp.where(on_grid, safe_patch % widths[picture] + 1, 0).astype(jnp.int32)
    segment = jnp.where(is_real, picture, IMAGES).astype(jnp.int32)
    return (segment, is_real.astype(jnp.int32), jnp.stack([row_pos, col_pos]), target)


def draw_segments(key, part):
    return layout(key)[0]


def draw_present(key, part):
    return layout(key)[1]


def draw_coords(key, part):
    return layout(key)[2]


def draw_owner_slot(key, part):
    return layout(key)[3]


def draw_tokens(key, part):
    base_key = jax.random.fold_in(key, 11)
    first_key, second_key, third_key = jax.random.split(base_key, 3)
    row_scale = 10.0 ** (jax.random.uniform(second_key, (TOKENS, 1), dtype=jnp.float32) - 0.5)
    column = jnp.arange(D, dtype=jnp.float32) / D
    col_scale = 10.0 ** (0.5 * column[None, :] + 0.5 * jax.random.uniform(third_key, (1, D), dtype=jnp.float32) - 0.5)
    noise = jnp.clip(jax.random.normal(first_key, (TOKENS, D), dtype=jnp.float32), -5.0, 5.0)
    result = noise * row_scale * col_scale
    return result.astype(jnp.bfloat16)


def draw_w_qkv(key, part):
    base_key = jax.random.fold_in(key, 13)
    first_key = jax.random.fold_in(base_key, 0)
    block = jnp.clip(jax.random.normal(first_key, (D, HEADS, 3, HD), dtype=jnp.float32), -5.0, 5.0)
    return (block.reshape(D, HEADS * 3 * HD) * D ** (-0.5)).astype(jnp.bfloat16)


def level_of(own_key, shape, cuts, least, high):
    factor_of, own = 1.0, jax.random.fold_in(own_key, 6)
    for dim, blocks in cuts:
        draws = jnp.exp(jax.random.uniform(jax.random.fold_in(own, dim), (blocks,), jnp.float32, least / len(cuts), high / len(cuts)))
        factor_of = factor_of * jnp.repeat(draws, shape[dim] // blocks).reshape([-1 if axis == dim else 1 for axis in range(len(shape))])
    return factor_of


def normal_values(stream_key, shape, scale, reach, shards=(), kind=jnp.bfloat16):
    gain = level_of(stream_key, shape, shards, -0.22, 0.18) if shards else 1.0
    entries = jax.random.normal(stream_key, shape, jnp.float32) * scale * gain
    return jnp.minimum(jnp.maximum(entries, -reach), reach).astype(kind)


def setup_inputs(seed: int = 0) -> dict:
    keys = jax.random.split(jax.random.key(seed), 11)
    return {
        "tokens": draw_tokens(jax.random.fold_in(keys[10], 71), 0),
        "ln_gain": jnp.clip(1.0 + 0.18 * jax.random.normal(keys[1], (D,), jnp.float32), 0.1, 1.9),
        "ln_shift": normal_values(keys[2], (D,), 0.3, 4.0, ((0, 8),), jnp.float32),
        "w_qkv": draw_w_qkv(jax.random.fold_in(keys[10], 71), 0),
        "w_out": normal_values(keys[4], (D, D), D ** -0.5, 0.09375, ((0, 16), (1, 8))),
        "layer_scale": jnp.clip(jnp.exp(math.log(2.0) - 1.3862944 * jax.random.uniform(keys[5], (D,), jnp.float32) ** level_of(keys[5], (D,), ((0, 8),), -0.2, 0.2)), 0.5, 2.0),
        "segments": draw_segments(jax.random.fold_in(keys[10], 71), 0),
        "present": draw_present(jax.random.fold_in(keys[10], 71), 0),
        "coords": draw_coords(jax.random.fold_in(keys[10], 71), 0),
        "owner_slot": draw_owner_slot(jax.random.fold_in(keys[10], 71), 0),
    }


def rotate(values, row_pos, col_pos):
    quarter = values.shape[-1] // 4
    frequency = 100.0 ** (-jnp.arange(quarter, dtype=jnp.float32) / quarter)
    angles = jnp.concatenate([row_pos[:, None] * frequency[None, :], col_pos[:, None] * frequency[None, :]], axis=1)
    cosine = jnp.cos(angles)[:, None, :]
    sine_wave = jnp.sin(angles)[:, None, :]
    former = jnp.concatenate([values[..., :quarter], values[..., 2 * quarter:3 * quarter]], axis=-1)
    latter = jnp.concatenate([values[..., quarter:2 * quarter], values[..., 3 * quarter:]], axis=-1)
    new_former = former * cosine - latter * sine_wave
    new_latter = latter * cosine + former * sine_wave
    return jnp.concatenate([new_former[..., :quarter], new_latter[..., :quarter], new_former[..., quarter:], new_latter[..., quarter:]], axis=-1)

def normalize(values, totals, squares, ln_gain, ln_shift):
    average = totals / D
    spread = squares / D - average * average
    scale_inv = lax.rsqrt(spread + 1e-06)
    return ((values - average[:, None]) * scale_inv[:, None] * ln_gain + ln_shift).astype(jnp.bfloat16)

def attend(query_rows, key_rows, values, seg_rows, live_rows):
    scores = jnp.einsum('qhe,khe->hqk', query_rows.astype(jnp.float32), key_rows.astype(jnp.float32)) * HD ** (-0.5)
    allowed = (seg_rows[:, None] == seg_rows[None, :]) & (live_rows[None, :] == 1)
    scores = jnp.where(allowed[None], scores, -1e+30)
    highest = lax.optimization_barrier(jnp.max(scores, axis=-1, keepdims=True))
    weights = jnp.exp(scores - highest)
    probability = (weights / lax.optimization_barrier(jnp.sum(weights, axis=-1, keepdims=True))).astype(jnp.bfloat16)
    result = jnp.einsum('hqk,khe->qhe', probability.astype(jnp.float32), values.astype(jnp.float32))
    return (result * live_rows[:, None, None].astype(jnp.float32)).astype(jnp.bfloat16)

def group_step(pieces):
    return attend(pieces[0], pieces[1], pieces[2], pieces[3], pieces[4])

def reference(tokens, ln_gain, ln_shift, w_qkv, w_out, layer_scale, segments, present, coords, owner_slot):
    own_rows = tokens.astype(jnp.float32)
    normed = normalize(own_rows, lax.optimization_barrier(jnp.sum(own_rows, axis=1)), lax.optimization_barrier(jnp.sum(own_rows * own_rows, axis=1)), ln_gain, ln_shift)
    slot_count = owner_slot.shape[0]
    at_slot = jnp.zeros((slot_count,), jnp.int32).at[owner_slot].set(jnp.arange(slot_count, dtype=jnp.int32))
    placed = normed[at_slot]
    stripe_width = D // N_ROW
    mixed = jnp.zeros((slot_count, w_qkv.shape[1]), jnp.float32)
    for stripe in range(N_ROW):
        start_col = stripe * stripe_width
        product = jnp.dot(placed[:, start_col:start_col + stripe_width], w_qkv[start_col:start_col + stripe_width], preferred_element_type=jnp.float32)
        rounded = lax.optimization_barrier(product.astype(jnp.bfloat16))
        mixed = mixed + rounded.astype(jnp.float32)
    mixed = mixed.reshape(slot_count, HEADS, 3, HD)
    row_pos = coords[0][at_slot].astype(jnp.float32)
    col_pos = coords[1][at_slot].astype(jnp.float32)
    query_rows = rotate(mixed[:, :, 0], row_pos, col_pos).astype(jnp.bfloat16)
    key_rows = rotate(mixed[:, :, 1], row_pos, col_pos).astype(jnp.bfloat16)
    values = mixed[:, :, 2].astype(jnp.bfloat16)
    seg_slot = segments[at_slot]
    live_slot = present[at_slot]
    groups = slot_count // TOK_ROW
    pieces = (query_rows.reshape(groups, TOK_ROW, HEADS, HD), key_rows.reshape(groups, TOK_ROW, HEADS, HD), values.reshape(groups, TOK_ROW, HEADS, HD), seg_slot.reshape(groups, TOK_ROW), live_slot.reshape(groups, TOK_ROW))
    attended = lax.map(group_step, pieces).reshape(slot_count, HEADS * HD)
    projected = jnp.dot(attended[owner_slot], w_out, preferred_element_type=jnp.float32)
    return (own_rows + layer_scale * projected).astype(jnp.bfloat16)
```

```python
import jax
import jax.numpy as jnp
from jax import lax
from jax.sharding import PartitionSpec as P

D = 4096
HD = 128


def rotate(values, row_pos, col_pos):
    quarter = values.shape[-1] // 4
    frequency = 100.0 ** (-jnp.arange(quarter, dtype=jnp.float32) / quarter)
    angles = jnp.concatenate(
        [row_pos[:, None] * frequency[None, :], col_pos[:, None] * frequency[None, :]], axis=1
    )
    cosine = jnp.cos(angles)[:, None, :]
    sine_wave = jnp.sin(angles)[:, None, :]
    former = jnp.concatenate(
        [values[..., :quarter], values[..., 2 * quarter : 3 * quarter]], axis=-1
    )
    latter = jnp.concatenate(
        [values[..., quarter : 2 * quarter], values[..., 3 * quarter :]], axis=-1
    )
    new_former = former * cosine - latter * sine_wave
    new_latter = latter * cosine + former * sine_wave
    return jnp.concatenate(
        [
            new_former[..., :quarter],
            new_latter[..., :quarter],
            new_former[..., quarter:],
            new_latter[..., quarter:],
        ],
        axis=-1,
    )


def normalize(values, totals, squares, ln_gain, ln_shift):
    average = totals / D
    spread = squares / D - average * average
    scale_inv = lax.rsqrt(spread + 1e-06)
    return ((values - average[:, None]) * scale_inv[:, None] * ln_gain + ln_shift).astype(
        jnp.bfloat16
    )


def local(
    tokens, ln_gain, ln_shift, w_qkv, w_out, layer_scale, segments, present, coords, owner_slot
):
    own_rows = tokens.astype(jnp.float32)
    totals, squares = lax.psum(
        (jnp.sum(own_rows, axis=1), jnp.sum(own_rows * own_rows, axis=1)), "row"
    )
    normed = normalize(own_rows, totals, squares, ln_gain, ln_shift)
    gathered = lax.all_gather(normed, "col", axis=0, tiled=True)
    count = gathered.shape[0]
    n_row = lax.axis_size("row")
    me = lax.axis_index("row")
    group_rows = count // n_row
    mixed = lax.psum_scatter(
        jnp.dot(gathered, w_qkv, preferred_element_type=jnp.float32).astype(jnp.bfloat16),
        "row",
        scatter_dimension=0,
        tiled=True,
    ).astype(jnp.float32)
    heads_here = w_qkv.shape[1] // (3 * HD)
    mixed = mixed.reshape(group_rows, heads_here, 3, HD)
    halo = group_rows // 2

    def own(values, before=0, after=0):
        padded = jnp.pad(values, (halo, halo), constant_values=-1)
        start = me * group_rows + halo - before
        return lax.dynamic_slice_in_dim(padded, start, group_rows + before + after, 0)

    row_pos = own(coords[0]).astype(jnp.float32)
    col_pos = own(coords[1]).astype(jnp.float32)
    seg_rows = own(segments)
    live_rows = own(present)
    seg_keys = own(segments, halo, halo)
    live_keys = own(present, halo, halo)
    query_rows = rotate(mixed[:, :, 0], row_pos, col_pos).astype(jnp.bfloat16)
    key_rows = rotate(mixed[:, :, 1], row_pos, col_pos).astype(jnp.bfloat16)
    values = mixed[:, :, 2].astype(jnp.bfloat16)
    both = jnp.stack([key_rows, values])
    up = [(k, (k + 1) % n_row) for k in range(n_row)]
    down = [((k + 1) % n_row, k) for k in range(n_row)]
    before = lax.ppermute(both[:, group_rows - halo :], "row", up)
    after = lax.ppermute(both[:, :halo], "row", down)
    both = jnp.concatenate([before, both, after], axis=1)
    scores = jnp.einsum(
        "qhe,khe->hqk", query_rows, both[0], preferred_element_type=jnp.float32
    ) * HD ** (-0.5)
    allowed = (seg_rows[:, None] == seg_keys[None, :]) & (live_keys[None, :] == 1)
    scores = jnp.where(allowed[None], scores, -1e30)
    highest = jnp.max(scores, axis=-1, keepdims=True)
    weights = jnp.exp(scores - highest)
    probability = (weights / jnp.sum(weights, axis=-1, keepdims=True)).astype(jnp.bfloat16)
    result = jnp.einsum("hqk,khe->qhe", probability, both[1], preferred_element_type=jnp.float32)
    attended = (result * live_rows[:, None, None].astype(jnp.float32)).astype(jnp.bfloat16)
    attended = attended.reshape(group_rows, heads_here * HD)
    all_tokens = lax.all_gather(attended, "row", axis=0, tiled=True)
    projected = lax.psum_scatter(
        jnp.dot(all_tokens, w_out, preferred_element_type=jnp.float32).astype(jnp.bfloat16),
        "col",
        scatter_dimension=0,
        tiled=True,
    ).astype(jnp.float32)
    return (own_rows + layer_scale * projected).astype(jnp.bfloat16)


def solution(mesh):
    in_specs = (
        P("col", "row"),
        P("row"),
        P("row"),
        P("row", "col"),
        P("col", "row"),
        P("row"),
        P(),
        P(),
        P(),
        P(),
    )
    out_specs = P("col", "row")
    return jax.shard_map(local, mesh=mesh, in_specs=in_specs, out_specs=out_specs, check_vma=False)
```
